256 devices in a mesh: src: 32 (over z, y), obs: 8 (over x, core).
Axes of the slice: x: 4, y: 4, z: 8, core: 2. Of those that a mesh axis runs over, the one named last changes fastest.
Arguments:
- tiles: bfloat16 [32, 8, 8, 8, 128, 128], P('src', 'obs'), may hold values from -0.125 to 0.125
- tile_src: int32 [32, 8, 8], P('src', 'obs'), may hold values from 0 to 7
- tile_obs: int32 [32, 8, 8], P('src', 'obs'), may hold values from 0 to 31
- tile_off: int32 [32, 8, 8], P('src', 'obs'), may hold values from 0 to 32, as said below
- history: bfloat16 [8, 1, 32, 40, 32, 128], P(None, None, 'src'), may hold values from -6 to 6
- excitation: bfloat16 [2, 8, 1, 32, 32, 128], P(None, 'obs', None, 'src'), may hold values from -6 to 6
- inverse: bfloat16 [8, 1, 32, 128, 128], P('obs', None, 'src'), may hold values from -0.5 to 0.5
Outputs:
- currents: bfloat16 [2, 8, 1, 32, 32, 128], P(None, 'obs', None, 'src')
The draws below stay inside these ranges and needn't reach their ends.
Inputs may be any that keep to these rules, and one draw needn't show every extreme that they name: `tile_off`: the delay offset of every tile; the least and the largest offset occur in every draw.
All inputs are finite; a program needn't handle non-finite values.
Results may differ from the reference program's by a relative error of at most 0.012.
Values may be sent and summed in bfloat16 or wider, within the bound.
A program may use at most 64 MiB of HBM per device.

```python
import jax
import jax.numpy as jnp
from jax import lax

G = 128
R = 32
HIST = 40
TAPS = 8
TILE_DEV = 8
OWN = 1
STEPS = 2
N_SRC = 32
N_OBS = 8


def draw_tile_off(key, part):
    shape = (N_SRC, N_OBS, TILE_DEV)
    subkeys = jax.random.split(jax.random.fold_in(key, 7), 5)
    chosen = jax.random.randint(subkeys[0], shape, 0, 10)
    nearby = jax.random.randint(subkeys[1], shape, 1, 4)
    widely = jax.random.randint(subkeys[2], shape, 0, HIST - TAPS + 1)
    offsets = jnp.where(chosen < 4, 0, jnp.where(chosen < 8, nearby, widely)).astype(jnp.int32)
    flattened = offsets.reshape(-1)
    total_tiles = N_SRC * N_OBS * TILE_DEV
    first_place = jax.random.randint(subkeys[3], (), 0, total_tiles)
    second_place = (first_place + 1 + jax.random.randint(subkeys[4], (), 0, total_tiles - 1)) % total_tiles
    flattened = flattened.at[first_place].set(0)
    flattened = flattened.at[second_place].set(HIST - TAPS)
    return flattened.reshape(shape).astype(jnp.int32)


def set_ends(result, stream_key, smallest, largest):
    longest = result.shape.index(max(result.shape))
    spots = []
    for shift in (0, 1):
        where = [jax.random.randint(jax.random.fold_in(stream_key, axis), (), 0, length) for axis, length in enumerate(result.shape)]
        where[longest] = (where[longest] + shift) % result.shape[longest]
        spots.append(tuple(where))
    return result.at[spots[0]].set(smallest).at[spots[1]].set(largest)


def level_of(stream_key, dims, pieces, least, high):
    def one(position, blocks):
        heights = jax.random.uniform(jax.random.fold_in(jax.random.fold_in(stream_key, 6), position), (blocks,), jnp.float32, least / len(pieces), high / len(pieces))
        return jnp.repeat(jnp.exp(heights), dims[position] // blocks).reshape((-1,) + (1,) * (len(dims) - position - 1))

    level = one(*pieces[0])
    for cut in pieces[1:]:
        level = level * one(*cut)
    return level


def noise(rng, dims, spread, most, pieces=(), kind=jnp.bfloat16):
    loudness = level_of(rng, dims, pieces, -0.22, 0.18) if pieces else 1.0
    values = jax.random.normal(rng, dims, jnp.float32) * spread * loudness
    return jnp.minimum(jnp.maximum(values, -most), most).astype(kind)


def setup_inputs(seed: int = 0) -> dict:
    seeds = jax.random.split(jax.random.key(seed), 8)
    tiles = noise(seeds[0], (N_SRC, N_OBS, TILE_DEV, TAPS, G, G), (G * TAPS * TILE_DEV // 4) ** -0.5, 0.125, ((0, 32), (1, 8)))
    tile_src = set_ends(jax.random.randint(seeds[1], (N_SRC, N_OBS, TILE_DEV), 0, N_OBS * OWN), jax.random.fold_in(seeds[1], 1), 0, (N_OBS * OWN) - 1).astype(jnp.int32)
    tile_obs = set_ends(jax.random.randint(seeds[2], (N_SRC, N_OBS, TILE_DEV), 0, N_SRC * OWN), jax.random.fold_in(seeds[2], 1), 0, (N_SRC * OWN) - 1).astype(jnp.int32)
    tile_off = draw_tile_off(jax.random.fold_in(seeds[7], 71), 0)
    history = noise(seeds[4], (N_OBS, OWN, N_SRC, HIST, R, G), 1.0, 6.0, ((2, 32),))
    excitation = noise(seeds[5], (STEPS, N_OBS, OWN, N_SRC, R, G), 1.0, 6.0, ((1, 8), (3, 32)))
    inverse = noise(seeds[6], (N_OBS, OWN, N_SRC, G, G), G ** -0.5, 0.5, ((0, 8), (2, 32)))
    return dict(tiles=tiles, tile_src=tile_src, tile_obs=tile_obs, tile_off=tile_off, history=history, excitation=excitation, inverse=inverse)


def reference(tiles, tile_src, tile_obs, tile_off, history, excitation, inverse):
    zero = jnp.zeros((), jnp.int32)
    hist = history
    results = []
    for step in range(STEPS):
        def per_source(s_index):
            hs = lax.dynamic_index_in_dim(hist, s_index, 2, keepdims=False)
            hs = hs.reshape(N_OBS * OWN, HIST, R, G)
            blocks = lax.dynamic_index_in_dim(tiles, s_index, 0, keepdims=False)
            sources = lax.dynamic_index_in_dim(tile_src, s_index, 0, keepdims=False)
            offsets = lax.dynamic_index_in_dim(tile_off, s_index, 0, keepdims=False)
            targets = lax.dynamic_index_in_dim(tile_obs, s_index, 0, keepdims=False)

            def window(j_index, offset):
                return lax.dynamic_slice(hs, (j_index.astype(jnp.int32), offset.astype(jnp.int32), zero, zero), (1, TAPS, R, G))[0]

            windows = jax.vmap(jax.vmap(window))(sources, offsets)
            contrib = jnp.einsum("otarg,otagh->otrh", windows.astype(jnp.float32), blocks.astype(jnp.float32))
            onehot = (targets[..., None] == jnp.arange(N_SRC * OWN, dtype=jnp.int32)).astype(jnp.float32)
            return jnp.einsum("oti,otrh->oirh", onehot, contrib)

        def accumulate(total, s_index):
            return total + per_source(s_index), None

        total, _ = lax.scan(accumulate, jnp.zeros((N_OBS, N_SRC * OWN, R, G), jnp.float32), jnp.arange(N_SRC, dtype=jnp.int32))
        total = total.reshape(N_OBS, N_SRC, OWN, R, G).transpose(0, 2, 1, 3, 4)
        field = (excitation[step].astype(jnp.float32) - total).astype(jnp.bfloat16)
        newer = jnp.einsum("oksrg,oksgh->oksrh", field.astype(jnp.float32), inverse.astype(jnp.float32)).astype(jnp.bfloat16)
        results.append(newer)
        hist = jnp.concatenate([newer[:, :, :, None], hist[:, :, :, :-1]], axis=3)
    return jnp.stack(results)
```

```python
import jax
import jax.numpy as jnp
from jax import lax
from jax.experimental import pallas as pl
from jax.experimental.pallas import tpu as pltpu
from jax.sharding import PartitionSpec as P

G = 128
R = 32
HIST = 40
TAPS = 8
STEPS = 2
TILES = 8
NZ = 8
NY = 4
NO = 8
MESH = pl.DeviceIdType.MESH

DELTA = (4, 3, 5, 2, 6, 1, 7, 0)
PER = 2
CHUNKS = NZ // PER
NEAR = NZ - 1
Y_ORDER = (2, 1, 3)
O_ORDER = (4, 5, 2, 3, 6, 7, 1)


def kernel(
    tiles_hbm, src_ref, obs_ref, off_ref, hist_hbm, exc_hbm, inv_hbm, out_ref,
    tiles, hist, exc, inv, contrib, part, mine, y_in, z_out, z_in, news,
    load_sem, hist_sem, tile_sem, y_send, y_recv, z_send, z_recv, o_send, o_recv,
):
    src = lax.axis_index("src")
    obs = lax.axis_index("obs")
    z = lax.div(src, NY)
    y = lax.rem(src, NY)

    def y_peer(d):
        return z * NY + lax.rem(y + d, NY)

    def z_peer(k):
        return lax.rem(z + DELTA[k], NZ) * NY + y

    def o_peer(e):
        return lax.rem(obs + e, NO)

    loads = []
    for j in range(NO):
        loads.append(pltpu.make_async_copy(hist_hbm.at[j], hist.at[j], hist_sem.at[j]))
    for t in range(TILES):
        loads.append(pltpu.make_async_copy(tiles_hbm.at[t], tiles.at[t], tile_sem.at[t]))
    loads.append(pltpu.make_async_copy(exc_hbm, exc, load_sem.at[0]))
    loads.append(pltpu.make_async_copy(inv_hbm, inv, load_sem.at[1]))
    for load in loads:
        load.start()

    barrier = pltpu.get_barrier_semaphore()
    for k in range(NEAR):
        pl.semaphore_signal(barrier, inc=1, device_id={"src": z_peer(k)}, device_id_type=MESH)
    for d in Y_ORDER:
        pl.semaphore_signal(barrier, inc=1, device_id={"src": y_peer(d)}, device_id_type=MESH)
    for e in O_ORDER:
        pl.semaphore_signal(barrier, inc=1, device_id={"obs": o_peer(e)}, device_id_type=MESH)

    for load in loads:
        load.wait()

    def block(t):
        return tiles[t].reshape(TAPS * G, G)

    for t in range(TILES):
        seen = hist[src_ref[t], pl.ds(off_ref[t], TAPS)]
        wide = jnp.concatenate([seen[p] for p in range(TAPS)], axis=1)
        contrib[0, t] = jnp.dot(wide, block(t), preferred_element_type=jnp.float32)

    pl.semaphore_wait(barrier, NEAR + NY - 1 + NO - 1)

    def y_copy(step, chunk, d):
        span = pl.ds(chunk * PER, PER)
        return pltpu.make_async_remote_copy(
            src_ref=part.at[step, d - 1, span],
            dst_ref=y_in.at[step, d - 1, span],
            send_sem=y_send.at[step, chunk, d - 1],
            recv_sem=y_recv.at[step, chunk, d - 1],
            device_id={"src": y_peer(d)},
            device_id_type=MESH,
        )

    def z_copy(step, k):
        return pltpu.make_async_remote_copy(
            src_ref=z_out.at[step, k],
            dst_ref=z_in.at[step, k],
            send_sem=z_send.at[step, k],
            recv_sem=z_recv.at[step, k],
            device_id={"src": z_peer(k)},
            device_id_type=MESH,
        )

    def o_copy(e):
        return pltpu.make_async_remote_copy(
            src_ref=news.at[obs],
            dst_ref=news.at[obs],
            send_sem=o_send.at[e - 1],
            recv_sem=o_recv.at[e - 1],
            device_id={"obs": o_peer(e)},
            device_id_type=MESH,
        )

    def owned_sum(step, owner):
        total = jnp.where(obs_ref[0] == owner, contrib[step, 0], 0.0)
        for t in range(1, TILES):
            total = total + jnp.where(obs_ref[t] == owner, contrib[step, t], 0.0)
        return total

    def scatter(step):
        for chunk in range(CHUNKS):
            for d in Y_ORDER:
                for k in range(chunk * PER, chunk * PER + PER):
                    owner = lax.rem(z + DELTA[k], NZ) * NY + lax.rem(y + d, NY)
                    part[step, d - 1, k] = owned_sum(step, owner).astype(jnp.bfloat16)
                y_copy(step, chunk, d).start()
        for k in range(NZ):
            mine[step, k] = owned_sum(step, lax.rem(z + DELTA[k], NZ) * NY + y)

    def gather_sum(step):
        for chunk in range(CHUNKS):
            for d in Y_ORDER:
                y_copy(step, chunk, d).wait_recv()
            for k in range(chunk * PER, chunk * PER + PER):
                total = mine[step, k]
                for d in Y_ORDER:
                    total = total + y_in[step, d - 1, k].astype(jnp.float32)
                if k < NEAR:
                    z_out[step, k] = total.astype(jnp.bfloat16)
                    z_copy(step, k).start()
        for k in range(NEAR - 1, -1, -1):
            z_copy(step, k).wait_recv()
            total = total + z_in[step, k].astype(jnp.float32)
        return total

    def solve(step, scattered):
        field = (exc[step].astype(jnp.float32) - scattered).astype(jnp.bfloat16)
        newer = jnp.dot(field, inv[...], preferred_element_type=jnp.float32).astype(jnp.bfloat16)
        out_ref[step] = newer
        return newer

    scatter(0)
    for t in range(TILES):
        off = off_ref[t]
        before = hist[src_ref[t], pl.ds(jnp.maximum(off - 1, 0), 1)][0]
        before = jnp.where(off > 0, before, jnp.zeros_like(before))
        seen = hist[src_ref[t], pl.ds(off, TAPS - 1)]
        wide = jnp.concatenate([before] + [seen[p] for p in range(TAPS - 1)], axis=1)
        contrib[1, t] = jnp.dot(wide, block(t), preferred_element_type=jnp.float32)

    news[obs] = solve(0, gather_sum(0))
    for e in O_ORDER:
        o_copy(e).start()
    for e in O_ORDER:
        o_copy(e).wait_recv()
    for t in range(TILES):
        fresh = news[src_ref[t]]
        fresh = jnp.where(off_ref[t] == 0, fresh, jnp.zeros_like(fresh))
        contrib[1, t] += jnp.dot(fresh, tiles[t, 0], preferred_element_type=jnp.float32)
    scatter(1)
    solve(1, gather_sum(1))

    for step in range(STEPS):
        for chunk in range(CHUNKS):
            for d in Y_ORDER:
                y_copy(step, chunk, d).wait_send()
        for k in range(NEAR):
            z_copy(step, k).wait_send()
    for e in O_ORDER:
        o_copy(e).wait_send()


def local(tiles, tile_src, tile_obs, tile_off, history, excitation, inverse):
    hbm = pl.BlockSpec(memory_space=pl.ANY)
    smem = pl.BlockSpec(memory_space=pltpu.SMEM)
    bf16, f32 = jnp.bfloat16, jnp.float32
    dma = pltpu.SemaphoreType.DMA
    out = pl.pallas_call(
        kernel,
        out_shape=jax.ShapeDtypeStruct((STEPS, R, G), bf16),
        in_specs=[hbm, smem, smem, smem, hbm, hbm, hbm],
        out_specs=pl.BlockSpec(memory_space=pltpu.VMEM),
        scratch_shapes=[
            pltpu.VMEM((TILES, TAPS, G, G), bf16),
            pltpu.VMEM((NO, HIST, R, G), bf16),
            pltpu.VMEM((STEPS, R, G), bf16),
            pltpu.VMEM((G, G), bf16),
            pltpu.VMEM((STEPS, TILES, R, G), f32),
            pltpu.VMEM((STEPS, NY - 1, NZ, R, G), bf16),
            pltpu.VMEM((STEPS, NZ, R, G), f32),
            pltpu.VMEM((STEPS, NY - 1, NZ, R, G), bf16),
            pltpu.VMEM((STEPS, NEAR, R, G), bf16),
            pltpu.VMEM((STEPS, NEAR, R, G), bf16),
            pltpu.VMEM((NO, R, G), bf16),
            dma((2,)),
            dma((NO,)),
            dma((TILES,)),
            dma((STEPS, CHUNKS, NY - 1)),
            dma((STEPS, CHUNKS, NY - 1)),
            dma((STEPS, NEAR)),
            dma((STEPS, NEAR)),
            dma((NO - 1,)),
            dma((NO - 1,)),
        ],
        compiler_params=pltpu.CompilerParams(collective_id=0, has_side_effects=True),
        name="march",
    )(
        tiles.reshape(TILES, TAPS, G, G),
        tile_src.reshape(TILES),
        tile_obs.reshape(TILES),
        tile_off.reshape(TILES),
        history.reshape(NO, HIST, R, G),
        excitation.reshape(STEPS, R, G),
        inverse.reshape(G, G),
    )
    return out.reshape(STEPS, 1, 1, 1, R, G)


def solution(mesh):
    placed = (
        P("src", "obs", None, None, None, None),
        P("src", "obs", None),
        P("src", "obs", None),
        P("src", "obs", None),
        P(None, None, "src", None, None, None),
        P(None, "obs", None, "src", None, None),
        P("obs", None, "src", None, None),
    )
    return jax.shard_map(
        local,
        mesh=mesh,
        in_specs=placed,
        out_specs=P(None, "obs", None, "src", None, None),
        check_vma=False,
    )
```

```python
import jax
import jax.numpy as jnp
from jax import lax
from jax.experimental import pallas as pl
from jax.experimental.pallas import tpu as pltpu
from jax.sharding import PartitionSpec as P

G = 128
R = 32
HIST = 40
TAPS = 8
STEPS = 2
TILES = 8
NZ = 8
NY = 4
NO = 8
MESH = pl.DeviceIdType.MESH

DELTA = (4, 3, 5, 2, 6, 1, 7, 0)
PER = 2
CHUNKS = NZ // PER
NEAR = NZ - 1
Y_ORDER = (2, 1, 3)
O_ORDER = (4, 5, 2, 3, 6, 7, 1)


def kernel(
    tiles_hbm, src_hbm, obs_hbm, off_hbm, hist_hbm, exc_hbm, inv_hbm, out_ref,
    src_ref, obs_ref, off_ref, tiles, hist, exc, inv, contrib, part, mine, y_in, z_out, z_in, news,
    load_sem, hist_sem, tile_sem, y_send, y_recv, z_send, z_recv, o_send, o_recv,
):
    src = lax.axis_index("src")
    obs = lax.axis_index("obs")
    z = lax.div(src, NY)
    y = lax.rem(src, NY)

    def y_peer(d):
        return z * NY + lax.rem(y + d, NY)

    def z_peer(k):
        return lax.rem(z + DELTA[k], NZ) * NY + y

    def o_peer(e):
        return lax.rem(obs + e, NO)

    loads = [
        pltpu.make_async_copy(src_hbm, src_ref, load_sem.at[2]),
        pltpu.make_async_copy(obs_hbm, obs_ref, load_sem.at[3]),
        pltpu.make_async_copy(off_hbm, off_ref, load_sem.at[4]),
    ]
    for j in range(NO):
        loads.append(pltpu.make_async_copy(hist_hbm.at[j], hist.at[j], hist_sem.at[j]))
    for t in range(TILES):
        loads.append(pltpu.make_async_copy(tiles_hbm.at[t], tiles.at[t], tile_sem.at[t]))
    loads.append(pltpu.make_async_copy(exc_hbm, exc, load_sem.at[0]))
    loads.append(pltpu.make_async_copy(inv_hbm, inv, load_sem.at[1]))
    for load in loads:
        load.start()

    barrier = pltpu.get_barrier_semaphore()
    for k in range(NEAR):
        pl.semaphore_signal(barrier, inc=1, device_id={"src": z_peer(k)}, device_id_type=MESH)
    for d in Y_ORDER:
        pl.semaphore_signal(barrier, inc=1, device_id={"src": y_peer(d)}, device_id_type=MESH)
    for e in O_ORDER:
        pl.semaphore_signal(barrier, inc=1, device_id={"obs": o_peer(e)}, device_id_type=MESH)

    for load in loads:
        load.wait()

    def block(t):
        return tiles[t].reshape(TAPS * G, G)

    for t in range(TILES):
        seen = hist[src_ref[t], pl.ds(off_ref[t], TAPS)]
        wide = jnp.concatenate([seen[p] for p in range(TAPS)], axis=1)
        contrib[0, t] = jnp.dot(wide, block(t), preferred_element_type=jnp.float32)

    pl.semaphore_wait(barrier, NEAR + NY - 1 + NO - 1)

    def y_copy(step, chunk, d):
        span = pl.ds(chunk * PER, PER)
        return pltpu.make_async_remote_copy(
            src_ref=part.at[step, d - 1, span],
            dst_ref=y_in.at[step, d - 1, span],
            send_sem=y_send.at[step, chunk, d - 1],
            recv_sem=y_recv.at[step, chunk, d - 1],
            device_id={"src": y_peer(d)},
            device_id_type=MESH,
        )

    def z_copy(step, k):
        return pltpu.make_async_remote_copy(
            src_ref=z_out.at[step, k],
            dst_ref=z_in.at[step, k],
            send_sem=z_send.at[step, k],
            recv_sem=z_recv.at[step, k],
            device_id={"src": z_peer(k)},
            device_id_type=MESH,
        )

    def o_copy(e):
        return pltpu.make_async_remote_copy(
            src_ref=news.at[obs],
            dst_ref=news.at[obs],
            send_sem=o_send.at[e - 1],
            recv_sem=o_recv.at[e - 1],
            device_id={"obs": o_peer(e)},
            device_id_type=MESH,
        )

    def owned_sum(step, owner):
        total = jnp.where(obs_ref[0] == owner, contrib[step, 0], 0.0)
        for t in range(1, TILES):
            total = total + jnp.where(obs_ref[t] == owner, contrib[step, t], 0.0)
        return total

    def scatter(step):
        for chunk in range(CHUNKS):
            for d in Y_ORDER:
                for k in range(chunk * PER, chunk * PER + PER):
                    owner = lax.rem(z + DELTA[k], NZ) * NY + lax.rem(y + d, NY)
                    part[step, d - 1, k] = owned_sum(step, owner).astype(jnp.bfloat16)
                y_copy(step, chunk, d).start()
        for k in range(NZ):
            mine[step, k] = owned_sum(step, lax.rem(z + DELTA[k], NZ) * NY + y)

    def gather_sum(step):
        for chunk in range(CHUNKS):
            for d in Y_ORDER:
                y_copy(step, chunk, d).wait_recv()
            for k in range(chunk * PER, chunk * PER + PER):
                total = mine[step, k]
                for d in Y_ORDER:
                    total = total + y_in[step, d - 1, k].astype(jnp.float32)
                if k < NEAR:
                    z_out[step, k] = total.astype(jnp.bfloat16)
                    z_copy(step, k).start()
        for k in range(NEAR - 1, -1, -1):
            z_copy(step, k).wait_recv()
            total = total + z_in[step, k].astype(jnp.float32)
        return total

    def solve(step, scattered):
        field = (exc[step].astype(jnp.float32) - scattered).astype(jnp.bfloat16)
        newer = jnp.dot(field, inv[...], preferred_element_type=jnp.float32).astype(jnp.bfloat16)
        out_ref[step] = newer
        return newer

    scatter(0)
    for t in range(TILES):
        off = off_ref[t]
        before = hist[src_ref[t], pl.ds(jnp.maximum(off - 1, 0), 1)][0]
        before = jnp.where(off > 0, before, jnp.zeros_like(before))
        seen = hist[src_ref[t], pl.ds(off, TAPS - 1)]
        wide = jnp.concatenate([before] + [seen[p] for p in range(TAPS - 1)], axis=1)
        contrib[1, t] = jnp.dot(wide, block(t), preferred_element_type=jnp.float32)

    news[obs] = solve(0, gather_sum(0))
    for e in O_ORDER:
        o_copy(e).start()
    for e in O_ORDER:
        o_copy(e).wait_recv()
    for t in range(TILES):
        fresh = news[src_ref[t]]
        fresh = jnp.where(off_ref[t] == 0, fresh, jnp.zeros_like(fresh))
        contrib[1, t] += jnp.dot(fresh, tiles[t, 0], preferred_element_type=jnp.float32)
    scatter(1)
    solve(1, gather_sum(1))

    for step in range(STEPS):
        for chunk in range(CHUNKS):
            for d in Y_ORDER:
                y_copy(step, chunk, d).wait_send()
        for k in range(NEAR):
            z_copy(step, k).wait_send()
    for e in O_ORDER:
        o_copy(e).wait_send()


def local(tiles, tile_src, tile_obs, tile_off, history, excitation, inverse):
    hbm = pl.BlockSpec(memory_space=pltpu.HBM)
    smem = pl.BlockSpec(memory_space=pltpu.SMEM)
    bf16, f32 = jnp.bfloat16, jnp.float32
    dma = pltpu.SemaphoreType.DMA
    out = pl.pallas_call(
        kernel,
        out_shape=jax.ShapeDtypeStruct((STEPS, R, G), bf16),
        in_specs=[hbm, hbm, hbm, hbm, hbm, hbm, hbm],
        out_specs=pl.BlockSpec(memory_space=pltpu.VMEM),
        scratch_shapes=[
            pltpu.SMEM((TILES,), jnp.int32),
            pltpu.SMEM((TILES,), jnp.int32),
            pltpu.SMEM((TILES,), jnp.int32),
            pltpu.VMEM((TILES, TAPS, G, G), bf16),
            pltpu.VMEM((NO, HIST, R, G), bf16),
            pltpu.VMEM((STEPS, R, G), bf16),
            pltpu.VMEM((G, G), bf16),
            pltpu.VMEM((STEPS, TILES, R, G), f32),
            pltpu.VMEM((STEPS, NY - 1, NZ, R, G), bf16),
            pltpu.VMEM((STEPS, NZ, R, G), f32),
            pltpu.VMEM((STEPS, NY - 1, NZ, R, G), bf16),
            pltpu.VMEM((STEPS, NEAR, R, G), bf16),
            pltpu.VMEM((STEPS, NEAR, R, G), bf16),
            pltpu.VMEM((NO, R, G), bf16),
            dma((5,)),
            dma((NO,)),
            dma((TILES,)),
            dma((STEPS, CHUNKS, NY - 1)),
            dma((STEPS, CHUNKS, NY - 1)),
            dma((STEPS, NEAR)),
            dma((STEPS, NEAR)),
            dma((NO - 1,)),
            dma((NO - 1,)),
        ],
        compiler_params=pltpu.CompilerParams(collective_id=0, vmem_limit_bytes=14680064, has_side_effects=True),
        name="march",
    )(
        pltpu.with_memory_space_constraint(tiles.reshape(TILES, TAPS, G, G), pltpu.HBM),
        pltpu.with_memory_space_constraint(tile_src.reshape(TILES), pltpu.HBM),
        pltpu.with_memory_space_constraint(tile_obs.reshape(TILES), pltpu.HBM),
        pltpu.with_memory_space_constraint(tile_off.reshape(TILES), pltpu.HBM),
        pltpu.with_memory_space_constraint(history.reshape(NO, HIST, R, G), pltpu.HBM),
        pltpu.with_memory_space_constraint(excitation.reshape(STEPS, R, G), pltpu.HBM),
        pltpu.with_memory_space_constraint(inverse.reshape(G, G), pltpu.HBM),
    )
    return out.reshape(STEPS, 1, 1, 1, R, G)


def solution(mesh):
    placed = (
        P("src", "obs", None, None, None, None),
        P("src", "obs", None),
        P("src", "obs", None),
        P("src", "obs", None),
        P(None, None, "src", None, None, None),
        P(None, "obs", None, "src", None, None),
        P("obs", None, "src", None, None),
    )
    return jax.shard_map(
        local,
        mesh=mesh,
        in_specs=placed,
        out_specs=P(None, "obs", None, "src", None, None),
        check_vma=False,
    )
```

```python
import jax
import jax.numpy as jnp
from jax import lax
from jax.experimental import pallas as pl
from jax.experimental.pallas import tpu as pltpu
from jax.sharding import PartitionSpec as P

G = 128
R = 32
HIST = 40
TAPS = 8
STEPS = 2
TILES = 8
NZ = 8
NY = 4
NO = 8
MESH = pl.DeviceIdType.MESH

DELTA = (4, 3, 5, 2, 6, 1, 7, 0)
PER = 2
CHUNKS = NZ // PER
NEAR = NZ - 1
Y_BLOCKS = (NY - 1) * NZ
SENT = Y_BLOCKS + NEAR
NEWS = STEPS * SENT
Y_ORDER = (2, 1, 3)
O_ORDER = (4, 5, 2, 3, 6, 7, 1)


def kernel(
    tiles_hbm, src_hbm, obs_hbm, off_hbm, hist_hbm, exc_hbm, inv_hbm, out_ref,
    src_ref, obs_ref, off_ref, tiles, hist, exc, inv, contrib, sent, mine, y_in, z_in, news,
    load_sem, send_sem, y_recv, z_recv, o_recv,
):
    src = lax.axis_index("src")
    obs = lax.axis_index("obs")
    z = lax.div(src, NY)
    y = lax.rem(src, NY)

    def y_peer(d):
        return z * NY + lax.rem(y + d, NY)

    def z_peer(k):
        return lax.rem(z + DELTA[k], NZ) * NY + y

    def o_peer(e):
        return lax.rem(obs + e, NO)

    loads = [
        pltpu.make_async_copy(src_hbm, src_ref, load_sem.at[2]),
        pltpu.make_async_copy(obs_hbm, obs_ref, load_sem.at[3]),
        pltpu.make_async_copy(off_hbm, off_ref, load_sem.at[4]),
    ]
    loads.append(pltpu.make_async_copy(hist_hbm, hist, load_sem.at[5]))
    loads.append(pltpu.make_async_copy(tiles_hbm, tiles, load_sem.at[6]))
    loads.append(pltpu.make_async_copy(exc_hbm, exc, load_sem.at[0]))
    loads.append(pltpu.make_async_copy(inv_hbm, inv, load_sem.at[1]))
    for load in loads:
        load.start()

    barrier = pltpu.get_barrier_semaphore()
    for k in range(NEAR):
        pl.semaphore_signal(barrier, inc=1, device_id={"src": z_peer(k)}, device_id_type=MESH)
    for d in Y_ORDER:
        pl.semaphore_signal(barrier, inc=1, device_id={"src": y_peer(d)}, device_id_type=MESH)
    for e in O_ORDER:
        pl.semaphore_signal(barrier, inc=1, device_id={"obs": o_peer(e)}, device_id_type=MESH)

    for load in loads:
        load.wait()

    def block(t):
        return tiles[t].reshape(TAPS * G, G)

    for t in range(TILES):
        seen = hist[src_ref[t], pl.ds(off_ref[t], TAPS)]
        wide = jnp.concatenate([seen[p] for p in range(TAPS)], axis=1)
        contrib[0, t] = jnp.dot(wide, block(t), preferred_element_type=jnp.float32)

    pl.semaphore_wait(barrier, NEAR + NY - 1 + NO - 1)

    def y_slot(step, chunk, d):
        return step * SENT + (chunk * (NY - 1) + d - 1) * PER

    def z_slot(step, k):
        return step * SENT + Y_BLOCKS + k

    def send_y(step, chunk, d):
        pltpu.make_async_remote_copy(
            src_ref=sent.at[pl.ds(y_slot(step, chunk, d), PER)],
            dst_ref=y_in.at[step, chunk, d - 1],
            send_sem=send_sem,
            recv_sem=y_recv.at[step, chunk],
            device_id={"src": y_peer(d)},
            device_id_type=MESH,
        ).start()

    def send_z(step, k):
        pltpu.make_async_remote_copy(
            src_ref=sent.at[z_slot(step, k)],
            dst_ref=z_in.at[step, k],
            send_sem=send_sem,
            recv_sem=z_recv.at[step],
            device_id={"src": z_peer(k)},
            device_id_type=MESH,
        ).start()

    def send_o(e):
        pltpu.make_async_remote_copy(
            src_ref=sent.at[NEWS],
            dst_ref=news.at[obs],
            send_sem=send_sem,
            recv_sem=o_recv,
            device_id={"obs": o_peer(e)},
            device_id_type=MESH,
        ).start()

    def wait_all(ref, sem):
        pltpu.make_async_copy(ref, ref, sem).wait()

    def owned_sum(step, owner):
        total = jnp.where(obs_ref[0] == owner, contrib[step, 0], 0.0)
        for t in range(1, TILES):
            total = total + jnp.where(obs_ref[t] == owner, contrib[step, t], 0.0)
        return total

    def scatter(step):
        for chunk in range(CHUNKS):
            for d in Y_ORDER:
                for i in range(PER):
                    owner = lax.rem(z + DELTA[chunk * PER + i], NZ) * NY + lax.rem(y + d, NY)
                    sent[y_slot(step, chunk, d) + i] = owned_sum(step, owner).astype(jnp.bfloat16)
                send_y(step, chunk, d)
        for k in range(NZ):
            mine[step, k] = owned_sum(step, lax.rem(z + DELTA[k], NZ) * NY + y)

    def gather_sum(step):
        for chunk in range(CHUNKS):
            wait_all(y_in.at[step, chunk], y_recv.at[step, chunk])
            for i in range(PER):
                k = chunk * PER + i
                total = mine[step, k]
                for d in Y_ORDER:
                    total = total + y_in[step, chunk, d - 1, i].astype(jnp.float32)
                if k < NEAR:
                    sent[z_slot(step, k)] = total.astype(jnp.bfloat16)
                    send_z(step, k)
        wait_all(z_in.at[step], z_recv.at[step])
        for k in range(NEAR):
            total = total + z_in[step, k].astype(jnp.float32)
        return total

    def solve(step, scattered):
        field = (exc[step].astype(jnp.float32) - scattered).astype(jnp.bfloat16)
        newer = jnp.dot(field, inv[...], preferred_element_type=jnp.float32).astype(jnp.bfloat16)
        out_ref[step] = newer
        return newer

    scatter(0)
    for t in range(TILES):
        off = off_ref[t]
        before = hist[src_ref[t], pl.ds(jnp.maximum(off - 1, 0), 1)][0]
        before = jnp.where(off > 0, before, jnp.zeros_like(before))
        seen = hist[src_ref[t], pl.ds(off, TAPS - 1)]
        wide = jnp.concatenate([before] + [seen[p] for p in range(TAPS - 1)], axis=1)
        contrib[1, t] = jnp.dot(wide, block(t), preferred_element_type=jnp.float32)

    newer = solve(0, gather_sum(0))
    sent[NEWS] = newer
    for e in O_ORDER:
        send_o(e)
    news[obs] = newer
    wait_all(news.at[pl.ds(0, NO - 1)], o_recv)
    for t in range(TILES):
        fresh = news[src_ref[t]]
        fresh = jnp.where(off_ref[t] == 0, fresh, jnp.zeros_like(fresh))
        contrib[1, t] += jnp.dot(fresh, tiles[t, 0], preferred_element_type=jnp.float32)
    scatter(1)
    solve(1, gather_sum(1))

    wait_all(sent, send_sem)


def local(tiles, tile_src, tile_obs, tile_off, history, excitation, inverse):
    hbm = pl.BlockSpec(memory_space=pltpu.HBM)
    smem = pl.BlockSpec(memory_space=pltpu.SMEM)
    bf16, f32 = jnp.bfloat16, jnp.float32
    dma = pltpu.SemaphoreType.DMA
    out = pl.pallas_call(
        kernel,
        out_shape=jax.ShapeDtypeStruct((STEPS, R, G), bf16),
        in_specs=[hbm, hbm, hbm, hbm, hbm, hbm, hbm],
        out_specs=pl.BlockSpec(memory_space=pltpu.VMEM),
        scratch_shapes=[
            pltpu.SMEM((TILES,), jnp.int32),
            pltpu.SMEM((TILES,), jnp.int32),
            pltpu.SMEM((TILES,), jnp.int32),
            pltpu.VMEM((TILES, TAPS, G, G), bf16),
            pltpu.VMEM((NO, HIST, R, G), bf16),
            pltpu.VMEM((STEPS, R, G), bf16),
            pltpu.VMEM((G, G), bf16),
            pltpu.VMEM((STEPS, TILES, R, G), f32),
            pltpu.VMEM((NEWS + NO - 1, R, G), bf16),
            pltpu.VMEM((STEPS, NZ, R, G), f32),
            pltpu.VMEM((STEPS, CHUNKS, NY - 1, PER, R, G), bf16),
            pltpu.VMEM((STEPS, NEAR, R, G), bf16),
            pltpu.VMEM((NO, R, G), bf16),
            dma((7,)),
            dma(()),
            dma((STEPS, CHUNKS)),
            dma((STEPS,)),
            dma(()),
        ],
        compiler_params=pltpu.CompilerParams(collective_id=0, vmem_limit_bytes=14680064, has_side_effects=True),
        name="march",
    )(
        pltpu.with_memory_space_constraint(tiles.reshape(TILES, TAPS, G, G), pltpu.HBM),
        pltpu.with_memory_space_constraint(tile_src.reshape(TILES), pltpu.HBM),
        pltpu.with_memory_space_constraint(tile_obs.reshape(TILES), pltpu.HBM),
        pltpu.with_memory_space_constraint(tile_off.reshape(TILES), pltpu.HBM),
        pltpu.with_memory_space_constraint(history.reshape(NO, HIST, R, G), pltpu.HBM),
        pltpu.with_memory_space_constraint(excitation.reshape(STEPS, R, G), pltpu.HBM),
        pltpu.with_memory_space_constraint(inverse.reshape(G, G), pltpu.HBM),
    )
    return out.reshape(STEPS, 1, 1, 1, R, G)


def solution(mesh):
    placed = (
        P("src", "obs", None, None, None, None),
        P("src", "obs", None),
        P("src", "obs", None),
        P("src", "obs", None),
        P(None, None, "src", None, None, None),
        P(None, "obs", None, "src", None, None),
        P("obs", None, "src", None, None),
    )
    return jax.shard_map(
        local,
        mesh=mesh,
        in_specs=placed,
        out_specs=P(None, "obs", None, "src", None, None),
        check_vma=False,
    )
```
